32 devices in a mesh: sec: 8 (over z, y), tile: 4 (over x, core).
Axes of the slice: x: 2, y: 2, z: 4, core: 2. Of those that a mesh axis runs over, the one named last changes fastest.
Arguments:
- patches: bfloat16 [48, 8, 8, 128, 128], P('sec', 'tile'), may hold values from -6 to 6
- pair_flags: int32 [48, 3], P('sec'), may hold values 0 or 1
- nodes: float32 [2, 48, 8, 8], P(None, 'sec', 'tile'), may hold values from -6 to 6
Outputs:
- relaxed: float32 [2, 48, 8, 8], P(None, 'sec', 'tile')
- measured: float32 [2, 48, 3, 8, 8], P(None, 'sec', None, 'tile')
The draws below stay inside these ranges and needn't reach their ends.
Inputs may be any that keep to these rules, and one draw needn't show every extreme that they name: `pair_flags`: flags of pairs whose partner lies past the last section are ignored.
All inputs are finite; a program needn't handle non-finite values. No bound on the sum of `pair_flags` on one device may be relied on, other than what follows from the above.
Results may differ from the reference program's by a relative error of at most 0.0081.
Values may be sent and summed in bfloat16 or wider, within the bound.
A program may use at most 128 MiB of HBM per device.

```python
import math
import jax
import jax.numpy as jnp
from jax import lax

P_SIZE = 128
COLS = 8
OFFS = 3
SWEEPS = 8
SECTIONS = 48
ROWS = 8


def place_ends(drawn, rng, smallest, high):
    index_at = [jax.random.randint(jax.random.fold_in(rng, axis), (), 0, length) for axis, length in enumerate(drawn.shape)]
    longest = drawn.shape.index(max(drawn.shape))
    next_to = index_at[:longest] + [(index_at[longest] + 1) % drawn.shape[longest]] + index_at[longest + 1:]
    return drawn.at[tuple(index_at)].set(smallest).at[tuple(next_to)].set(high)


def steps_of(rng, shape, split, low, high):
    factor_of = 1.0
    for position, shards_of in split:
        heights = jax.random.uniform(jax.random.fold_in(jax.random.fold_in(rng, 6), position), (shards_of,), jnp.float32, low / len(split), high / len(split))
        factor_of = factor_of * jnp.repeat(jnp.exp(heights), shape[position] // shards_of).reshape((-1,) + (1,) * (len(shape) - 1 - position))
    return factor_of


def centred(own_key, dims, width, most, split=(), held_as=jnp.bfloat16):
    gain = steps_of(own_key, dims, split, -0.22, 0.18) if split else 1.0
    entries = jax.random.normal(own_key, dims, jnp.float32) * width * gain
    return jnp.minimum(jnp.maximum(entries, -most), most).astype(held_as)


def setup_inputs(seed: int = 0) -> dict:
    streams_of = jax.random.split(jax.random.key(seed), 4)
    patches = centred(streams_of[0], (SECTIONS, ROWS, COLS, P_SIZE, P_SIZE), 1.0, 6.0, ((0, 8), (1, 4)))
    pair_flags = place_ends((jax.random.randint(streams_of[1], (SECTIONS, OFFS), 0, 3) < 2).astype(jnp.int32), jax.random.fold_in(streams_of[1], 1), 0, 1)
    nodes = centred(streams_of[2], (2, SECTIONS, ROWS, COLS), 1.0, 6.0, ((1, 8), (2, 4)), jnp.float32)
    return {"patches": patches, "pair_flags": pair_flags, "nodes": nodes}


STEP_SIZE = 0.08
EPSILON = 1e-6


def transform_tables(length):
    index = jnp.arange(length, dtype=jnp.int32)
    phase = ((index[:, None] * index[None, :]) % length).astype(jnp.float32) * (2.0 * math.pi / length)
    cosine = jnp.cos(phase)
    sine = jnp.sin(phase)
    forward_first = jnp.concatenate([cosine, sine], axis=1).astype(jnp.bfloat16)
    forward_second = jnp.stack([jnp.stack([cosine, -sine], 1), jnp.stack([-sine, -cosine], 1)], 0).astype(jnp.bfloat16)
    inverse_first = jnp.stack([jnp.stack([cosine, sine], 1), jnp.stack([-sine, cosine], 1)], 0).astype(jnp.bfloat16)
    inverse_second = jnp.stack([cosine, -sine], 1).astype(jnp.bfloat16)
    shifts = jnp.where(index < length // 2, index, index - length).astype(jnp.float32)
    return forward_first, forward_second, inverse_first, inverse_second, shifts


def spectrum(block, tabs):
    length = block.shape[-1]
    half = jnp.einsum("...aj,jm->...am", block.astype(jnp.float32), tabs[0].astype(jnp.float32)).astype(jnp.bfloat16)
    half = half.reshape(half.shape[:-1] + (2, length))
    return jnp.einsum("rahj,...jhk->...rak", tabs[1].astype(jnp.float32), half.astype(jnp.float32)).astype(jnp.bfloat16)


def measure(first_spec, second_spec, weight, tabs):
    length = first_spec.shape[-1]
    left = first_spec.astype(jnp.float32)
    right = second_spec.astype(jnp.float32)
    real = left[..., 0, :, :] * right[..., 0, :, :] + left[..., 1, :, :] * right[..., 1, :, :]
    imag = left[..., 0, :, :] * right[..., 1, :, :] - left[..., 1, :, :] * right[..., 0, :, :]
    cross = jnp.stack([real, imag], axis=-3).astype(jnp.bfloat16)
    back = jnp.einsum("...qaj,qjrk->...rak", cross.astype(jnp.float32), tabs[2].astype(jnp.float32)).astype(jnp.bfloat16)
    corr = jnp.einsum("arj,...rjk->...ak", tabs[3].astype(jnp.float32), back.astype(jnp.float32)) * (1.0 / float(length) ** 3)
    power = corr * corr
    total = jnp.mean(power, axis=(-2, -1)) + EPSILON
    along_rows = jnp.mean(power * tabs[4][:, None], axis=(-2, -1))
    along_cols = jnp.mean(power * tabs[4][None, :], axis=(-2, -1))
    return jnp.stack([along_rows / total, along_cols / total], 0) * weight


def plane_force(u):
    rows = u.shape[2]
    cols = u.shape[3]
    row_place = jnp.arange(rows, dtype=jnp.int32)
    col_place = jnp.arange(cols, dtype=jnp.int32)
    has_up = (row_place > 0).astype(jnp.float32)[:, None]
    has_down = (row_place < rows - 1).astype(jnp.float32)[:, None]
    has_left = (col_place > 0).astype(jnp.float32)[None, :]
    has_right = (col_place < cols - 1).astype(jnp.float32)[None, :]
    zero_row = jnp.zeros_like(u[:, :, :1])
    zero_col = jnp.zeros_like(u[..., :1])
    above = jnp.concatenate([zero_row, u[:, :, :-1]], axis=2)
    below = jnp.concatenate([u[:, :, 1:], zero_row], axis=2)
    left = jnp.concatenate([zero_col, u[..., :-1]], axis=3)
    right = jnp.concatenate([u[..., 1:], zero_col], axis=3)
    return has_up * (above - u) + has_down * (below - u) + has_left * (left - u) + has_right * (right - u)


def reference(patches, pair_flags, nodes):
    tabs = transform_tables(P_SIZE)
    spectra = lax.map(lambda block: spectrum(block, tabs), patches)
    sections = patches.shape[0]
    offsets = jnp.arange(1, OFFS + 1, dtype=jnp.int32)
    placed = jnp.arange(sections, dtype=jnp.int32)
    weights = pair_flags.astype(jnp.float32) * ((placed[:, None] + offsets[None, :]) < sections).astype(jnp.float32)

    def per_section(index):
        own = lax.dynamic_index_in_dim(spectra, index, 0, keepdims=False)
        results = []
        for step in range(OFFS):
            where = jnp.minimum(index + step + 1, sections - 1).astype(jnp.int32)
            other = lax.dynamic_index_in_dim(spectra, where, 0, keepdims=False)
            results.append(measure(own, other, weights[index, step], tabs))
        return jnp.stack(results, axis=1)

    measured = lax.map(per_section, placed)
    measured = jnp.transpose(measured, (1, 0, 2, 3, 4))
    u = nodes
    for sweep in range(SWEEPS):
        spring = jnp.zeros_like(u)
        for step in range(OFFS):
            offset = step + 1
            ahead = jnp.concatenate([u[:, offset:], jnp.zeros_like(u[:, :offset])], axis=1)
            resid = weights[None, :, step, None, None] * (ahead - u - measured[:, :, step])
            spring = spring + resid - jnp.concatenate([jnp.zeros_like(resid[:, :offset]), resid[:, :sections - offset]], axis=1)
        u = u + STEP_SIZE * (plane_force(u) + spring)
    return u, measured
```

```python
import functools
import math

import jax
import jax.numpy as jnp
import numpy as np
from jax import lax
from jax.experimental import pallas as pl
from jax.experimental.pallas import tpu as pltpu
from jax.sharding import PartitionSpec as P

SWEEPS = 8
STEP_SIZE = 0.08
EPSILON = 1e-06
LANES = 128
TILE = 8
MESH = pl.DeviceIdType.MESH


def tables(n):
    h = n // 2
    k = np.arange(n)
    phase = (k[:, None] * k[None, :] % n) * (2.0 * math.pi / n)
    c = np.asarray(np.cos(phase), np.float32).astype(jnp.bfloat16).astype(np.float32)
    s = np.asarray(np.sin(phase), np.float32).astype(jnp.bfloat16).astype(np.float32)
    first = np.concatenate([c, s], 1)
    part = h + TILE
    second = np.zeros((2 * part, 2 * n), np.float32)
    second[: h + 1, :n] = c[: h + 1]
    second[: h + 1, n:] = -s[: h + 1]
    second[part : part + h + 1, :n] = -s[: h + 1]
    second[part : part + h + 1, n:] = -c[: h + 1]
    inverse = np.concatenate([np.concatenate([c, s], 1), np.concatenate([-s, c], 1)], 0)
    order = (np.arange(n) - h) % n
    last = np.zeros((n, n), np.float32)
    last[:, 0] = c[order, 0]
    last[:, 1:h] = 2.0 * c[order, 1:h]
    last[:, h] = c[order, h]
    last[:, h + 1 :] = -2.0 * s[order, 1:h]
    last *= 1.0 / float(n) ** 3
    weigh = np.zeros((TILE, n), np.float32)
    weigh[0] = 1.0
    weigh[1] = np.where(k < h, k, k - n)
    low = lambda a: np.asarray(a).astype(jnp.bfloat16)
    return low(first), low(second), low(inverse), low(last), weigh


def spectra(x, first, second, put):
    cols, n = x.shape[0], x.shape[-1]
    half = jnp.dot(x.reshape(cols * n, n), first, preferred_element_type=jnp.float32)
    half = half.astype(jnp.bfloat16)
    for c in range(0, cols, 2):
        sides = []
        for d in (c, c + 1):
            mine = half[d * n : (d + 1) * n]
            sides.append(jnp.concatenate([mine[:, :n], mine[:, n:]], axis=0))
        spec = jnp.dot(
            second, jnp.concatenate(sides, axis=1), preferred_element_type=jnp.float32
        )
        put(c, spec[:, :n])
        put(c + 1, spec[:, n:])


def pairs(get_a, get_b, cols, n, inverse, last, weigh, sums):
    h = n // 2
    part = h + TILE
    crosses = []
    for c in range(cols):
        a, b = get_a(c), get_b(c)
        ar, ai, br, bi = a[:part], a[part:], b[:part], b[part:]
        real = ar * br + ai * bi
        imag = ar * bi - ai * br
        real_top = real[:TILE] - imag[h:]
        imag_top = imag[:TILE] + real[h:]
        real = jnp.concatenate([real_top, real[TILE:h]], axis=0).astype(jnp.bfloat16)
        imag = jnp.concatenate([imag_top, imag[TILE:h]], axis=0).astype(jnp.bfloat16)
        crosses.append(jnp.concatenate([real, imag], axis=1))
    back = jnp.dot(
        jnp.concatenate(crosses, axis=0), inverse, preferred_element_type=jnp.float32
    ).astype(jnp.bfloat16)
    place = lax.broadcasted_iota(jnp.int32, (TILE, 1), 0).astype(jnp.float32) + float(h)
    for c in range(0, cols, 2):
        sides = []
        for d in (c, c + 1):
            mine = back[d * h : (d + 1) * h]
            sides.append(jnp.concatenate([mine[:, :n], mine[:, n:]], axis=0))
        corr = jnp.dot(last, jnp.concatenate(sides, axis=1), preferred_element_type=jnp.float32)
        power = corr * corr
        total = power[:TILE]
        ramp = total
        for t in range(1, n // TILE):
            total = total + power[t * TILE : (t + 1) * TILE]
            ramp = ramp + total
        shifted = place * total - float(TILE) * ramp
        total = jnp.sum(total, axis=0, keepdims=True)
        shifted = jnp.sum(shifted, axis=0, keepdims=True)
        for d in (0, 1):
            sums[c + d : c + d + 1, :] = shifted[:, d * n : (d + 1) * n]
            sums[cols + c + d : cols + c + d + 1, :] = total[:, d * n : (d + 1) * n]
    return lax.dot_general(
        weigh,
        sums[...],
        (((1,), (1,)), ((), ())),
        precision=lax.Precision.HIGHEST,
        preferred_element_type=jnp.float32,
    )


def own_kernel(reach, x, first, second, inverse, last, weigh, red, tail, spec, sums):
    row = pl.program_id(0)
    step = pl.program_id(1)
    local = pl.num_programs(1)
    cols, n = x.shape[2], x.shape[-1]

    def put(c, value):
        spec[step, c] = value

        @pl.when(step >= local - reach)
        def _():
            tail[jnp.maximum(step - (local - reach), 0), 0, c] = value.astype(tail.dtype)

    spectra(x[0, 0], first[...], second[...], put)

    def body(offset, carry):
        red[step - offset, offset - 1, row] = pairs(
            lambda c: spec[step - offset, c],
            lambda c: spec[step, c],
            cols, n, inverse[...], last[...], weigh[...], sums,
        )
        return carry

    lax.fori_loop(1, jnp.minimum(step, reach) + 1, body, 0)


def far_kernel(count, x, first, second, inverse, last, weigh, *rest):
    own, red, spec, sums = rest[:count], rest[count], rest[count + 1], rest[count + 2]
    cols, n = x.shape[2], x.shape[-1]

    def put(c, value):
        spec[c] = value

    spectra(x[0, 0], first[...], second[...], put)
    for item in range(count):
        red[item, 0] = pairs(
            lambda c: own[item][0, 0, c].astype(jnp.float32),
            lambda c: spec[c],
            cols, n, inverse[...], last[...], weigh[...], sums,
        )


def fixed(array):
    zeros = (0,) * array.ndim
    return pl.BlockSpec(array.shape, lambda *_: zeros)


def cost(patches, pair_count, n):
    return pl.CostEstimate(
        flops=(patches + pair_count) * 24 * n**3,
        bytes_accessed=patches * n * n * 16,
        transcendentals=0,
    )


def relax_kernel(sizes, base, out, slots, field, weight, send, recv):
    groups, tiles, local, reach, span, grid_rows, grid_cols = sizes
    half = LANES // 2
    sec = lax.axis_index("sec")
    tile = lax.axis_index("tile")
    me = sec * tiles + tile
    count = groups * tiles

    def place(index):
        return (index // tiles, index % tiles)

    barrier = pltpu.get_barrier_semaphore()

    def greet(d, carry):
        pl.semaphore_signal(
            barrier, inc=1, device_id=place((me + d) % count), device_id_type=MESH
        )
        return carry

    lax.fori_loop(1, count, greet, 0)
    pl.semaphore_wait(barrier, count - 1)

    def copy(slot, peer):
        return pltpu.make_async_remote_copy(
            src_ref=base,
            dst_ref=slots.at[slot],
            send_sem=send.at[peer],
            recv_sem=recv.at[slot],
            device_id=place(peer),
            device_id_type=MESH,
        )

    def start(d, carry):
        copy(me, (me + d) % count).start()
        return carry

    lax.fori_loop(1, count, start, 0)
    slots[me] = base[...]

    def finish(d, carry):
        peer = (me + d) % count
        copy(peer, peer).wait_recv()
        copy(me, peer).wait_send()
        return carry

    lax.fori_loop(1, count, finish, 0)

    lane = lax.broadcasted_iota(jnp.int32, (TILE, LANES), 1)
    sub = lax.broadcasted_iota(jnp.int32, (TILE, LANES), 0)
    owner = lane % half // span
    for g in range(groups):
        blocks = [slots[g * tiles + t] for t in range(tiles)]
        for v in range(reach + 1):
            value = jnp.zeros((TILE, LANES), jnp.float32)
            for t in range(tiles):
                moved = blocks[t]
                if t != v:
                    moved = pltpu.roll(moved, (t - v) * span % LANES, 1)
                value = jnp.where(owner == t, moved, value)
            field[v, g * local : (g + 1) * local, :] = value[:local]
        row = jnp.broadcast_to(blocks[0][local : local + 1], (TILE, LANES))
        for v in range(reach):
            w = jnp.sum(jnp.where(lane == sub * reach + v, row, 0.0), axis=1, keepdims=True)
            w = jnp.broadcast_to(w, (TILE, LANES))
            weight[v, g * local : (g + 1) * local, :] = w[:local]

    total = groups * local
    spot = lax.broadcasted_iota(jnp.int32, (total, LANES), 1) % half
    across = spot % grid_cols
    down = spot // grid_cols
    one = lambda mask: mask.astype(jnp.float32)
    left, right = one(across > 0), one(across < grid_cols - 1)
    up, below = one(down > 0), one(down < grid_rows - 1)

    def sweep(_, u):
        plane = (
            up * (pltpu.roll(u, grid_cols, 1) - u)
            + below * (pltpu.roll(u, LANES - grid_cols, 1) - u)
            + left * (pltpu.roll(u, 1, 1) - u)
            + right * (pltpu.roll(u, LANES - 1, 1) - u)
        )
        spring = jnp.zeros_like(u)
        for v in range(reach):
            o = v + 1
            r = weight[v] * (pltpu.roll(u, total - o, 0) - u - field[v])
            spring = spring + r - pltpu.roll(r, o, 0)
        return u + STEP_SIZE * (plane + spring)

    state = lax.fori_loop(0, SWEEPS, sweep, field[reach])
    field[reach] = state
    mine = field[reach, pl.ds(sec * local, local), :]
    mine = jnp.concatenate([mine, jnp.zeros((TILE - local, LANES), jnp.float32)], axis=0)
    out[...] = pltpu.roll(mine, (LANES - tile * span) % LANES, 1)


def shards(patches, pair_flags, nodes):
    local, rows, cols, n = patches.shape[:4]
    reach = pair_flags.shape[1]
    groups, tiles = lax.axis_size("sec"), lax.axis_size("tile")
    part = n // 2 + TILE
    tabs = [jnp.asarray(t) for t in tables(n)]
    tab_specs = [fixed(t) for t in tabs]
    back_by_one = [(i, i - 1) for i in range(1, groups)]
    ahead = [lax.ppermute(patches[r : r + 1], "sec", back_by_one) for r in range(reach)]

    patch_block = (1, 1, cols, n, n)
    red, tail = pl.pallas_call(
        functools.partial(own_kernel, reach),
        grid=(rows, local),
        in_specs=[pl.BlockSpec(patch_block, lambda i, s: (s, i, 0, 0, 0))] + tab_specs,
        out_specs=[
            pl.BlockSpec((local, reach, rows, TILE, 2 * cols), lambda i, s: (0, 0, 0, 0, 0)),
            pl.BlockSpec((reach, 1, cols, 2 * part, n), lambda i, s: (0, i, 0, 0, 0)),
        ],
        out_shape=[
            jax.ShapeDtypeStruct((local, reach, rows, TILE, 2 * cols), jnp.float32),
            jax.ShapeDtypeStruct((reach, rows, cols, 2 * part, n), jnp.bfloat16),
        ],
        scratch_shapes=[
            pltpu.VMEM((local, cols, 2 * part, n), jnp.float32),
            pltpu.VMEM((2 * cols, n), jnp.float32),
        ],
        compiler_params=pltpu.CompilerParams(
            dimension_semantics=("arbitrary", "arbitrary"), vmem_limit_bytes=40 << 20
        ),
        cost_estimate=cost(local * rows * cols, (reach * local - reach * (reach + 1) // 2) * rows * cols, n),
        name="own_pairs",
    )(patches, *tabs)

    grid = {}
    for r in range(reach):
        count = reach - r
        own_specs = [
            pl.BlockSpec((1, 1, cols, 2 * part, n), functools.partial(lambda k, i: (k, i, 0, 0, 0), k))
            for k in range(r, reach)
        ]
        far = pl.pallas_call(
            functools.partial(far_kernel, count),
            grid=(rows,),
            in_specs=[pl.BlockSpec(patch_block, lambda i: (0, i, 0, 0, 0))] + tab_specs + own_specs,
            out_specs=pl.BlockSpec((count, 1, TILE, 2 * cols), lambda i: (0, i, 0, 0)),
            out_shape=jax.ShapeDtypeStruct((count, rows, TILE, 2 * cols), jnp.float32),
            scratch_shapes=[
                pltpu.VMEM((cols, 2 * part, n), jnp.float32),
                pltpu.VMEM((2 * cols, n), jnp.float32),
            ],
            compiler_params=pltpu.CompilerParams(
                dimension_semantics=("arbitrary",), vmem_limit_bytes=24 << 20
            ),
            cost_estimate=cost(rows * cols, count * rows * cols, n),
            name=f"far_pairs_{r}",
        )(ahead[r], *tabs, *([tail] * count))
        for item in range(count):
            section = local - reach + r + item
            grid[section, local + r - section] = far[item]
    stats = jnp.stack(
        [
            jnp.stack([grid.get((s, o), red[s, o - 1]) for o in range(1, reach + 1)], 0)
            for s in range(local)
        ],
        0,
    )

    placed = lax.axis_index("sec") * local + jnp.arange(local, dtype=jnp.int32)
    offsets = jnp.arange(1, reach + 1, dtype=jnp.int32)
    weights = pair_flags.astype(jnp.float32) * (
        placed[:, None] + offsets[None, :] < groups * local
    ).astype(jnp.float32)
    area = float(n * n)
    total = stats[..., 0, cols:] / area + EPSILON
    ratio = jnp.stack([stats[..., 0, :cols], stats[..., 1, cols:]], 0) / area / total
    measured = ratio * weights[None, :, :, None, None]

    span = rows * cols
    lanes = jnp.concatenate(
        [
            jnp.transpose(measured, (1, 0, 2, 3, 4)).reshape(local, 2, reach * span),
            jnp.transpose(nodes, (1, 0, 2, 3)).reshape(local, 2, span),
        ],
        axis=2,
    )
    lanes = jnp.pad(lanes, ((0, 0), (0, 0), (0, LANES // 2 - (reach + 1) * span)))
    flat = jnp.pad(weights.reshape(1, local * reach), ((0, 0), (0, LANES - local * reach)))
    base = jnp.concatenate([lanes.reshape(local, LANES), flat], axis=0)
    base = jnp.pad(base, ((0, TILE - local - 1), (0, 0)))

    sizes = (groups, tiles, local, reach, span, tiles * rows, cols)
    vmem = pl.BlockSpec(memory_space=pltpu.VMEM)
    moved = pl.pallas_call(
        functools.partial(relax_kernel, sizes),
        in_specs=[vmem],
        out_specs=vmem,
        out_shape=jax.ShapeDtypeStruct((TILE, LANES), jnp.float32),
        scratch_shapes=[
            pltpu.VMEM((groups * tiles, TILE, LANES), jnp.float32),
            pltpu.VMEM((reach + 1, groups * local, LANES), jnp.float32),
            pltpu.VMEM((reach, groups * local, LANES), jnp.float32),
            pltpu.SemaphoreType.DMA((groups * tiles,)),
            pltpu.SemaphoreType.DMA((groups * tiles,)),
        ],
        compiler_params=pltpu.CompilerParams(
            collective_id=0, has_side_effects=True, vmem_limit_bytes=24 << 20
        ),
        name="relax",
    )(base)
    positions = moved[:local].reshape(local, 2, LANES // 2)[:, :, :span]
    positions = jnp.transpose(positions.reshape(local, 2, rows, cols), (1, 0, 2, 3))
    return (positions, measured)


def solution(mesh):
    placed = (P("sec", "tile", None, None, None), P("sec", None), P(None, "sec", "tile", None))
    return jax.shard_map(
        shards,
        mesh=mesh,
        in_specs=placed,
        out_specs=(P(None, "sec", "tile", None), P(None, "sec", None, "tile", None)),
        check_vma=False,
    )
```

```python
import functools
import math

import jax
import jax.numpy as jnp
import numpy as np
from jax import lax
from jax.experimental import pallas as pl
from jax.experimental.pallas import tpu as pltpu
from jax.sharding import PartitionSpec as P

SWEEPS = 8
STEP_SIZE = 0.08
EPSILON = 1e-06
LANES = 128
TILE = 8
MESH = pl.DeviceIdType.MESH


def tables(n):
    h = n // 2
    k = np.arange(n)
    phase = (k[:, None] * k[None, :] % n) * (2.0 * math.pi / n)
    c = np.asarray(np.cos(phase), np.float32).astype(jnp.bfloat16).astype(np.float32)
    s = np.asarray(np.sin(phase), np.float32).astype(jnp.bfloat16).astype(np.float32)
    first = np.concatenate([c, s], 1)
    part = h + TILE
    second = np.zeros((2 * part, 2 * n), np.float32)
    second[: h + 1, :n] = c[: h + 1]
    second[: h + 1, n:] = -s[: h + 1]
    second[part : part + h + 1, :n] = -s[: h + 1]
    second[part : part + h + 1, n:] = -c[: h + 1]
    inverse = np.concatenate([np.concatenate([c, s], 1), np.concatenate([-s, c], 1)], 0)
    order = (np.arange(n) - h) % n
    last = np.zeros((n, n), np.float32)
    last[:, 0] = c[order, 0]
    last[:, 1:h] = 2.0 * c[order, 1:h]
    last[:, h] = c[order, h]
    last[:, h + 1 :] = -2.0 * s[order, 1:h]
    last *= 1.0 / float(n) ** 3
    weigh = np.zeros((TILE, n), np.float32)
    weigh[0] = 1.0
    weigh[1] = np.where(k < h, k, k - n)
    low = lambda a: np.asarray(a).astype(jnp.bfloat16)
    return low(first), low(second), low(inverse), low(last), weigh


def spectra(x, first, second, put):
    cols, n = x.shape[0], x.shape[-1]
    half = jnp.dot(x.reshape(cols * n, n), first, preferred_element_type=jnp.float32)
    half = half.astype(jnp.bfloat16)
    for c in range(0, cols, 2):
        sides = []
        for d in (c, c + 1):
            mine = half[d * n : (d + 1) * n]
            sides.append(jnp.concatenate([mine[:, :n], mine[:, n:]], axis=0))
        spec = jnp.dot(
            second, jnp.concatenate(sides, axis=1), preferred_element_type=jnp.float32
        )
        put(c, spec[:, :n])
        put(c + 1, spec[:, n:])


def pairs(get_a, get_b, cols, n, inverse, last, weigh, sums):
    h = n // 2
    part = h + TILE
    crosses = []
    for c in range(cols):
        a, b = get_a(c), get_b(c)
        ar, ai, br, bi = a[:part], a[part:], b[:part], b[part:]
        real = ar * br + ai * bi
        imag = ar * bi - ai * br
        real_top = real[:TILE] - imag[h:]
        imag_top = imag[:TILE] + real[h:]
        real = jnp.concatenate([real_top, real[TILE:h]], axis=0).astype(jnp.bfloat16)
        imag = jnp.concatenate([imag_top, imag[TILE:h]], axis=0).astype(jnp.bfloat16)
        crosses.append(jnp.concatenate([real, imag], axis=1))
    back = jnp.dot(
        jnp.concatenate(crosses, axis=0), inverse, preferred_element_type=jnp.float32
    ).astype(jnp.bfloat16)
    place = lax.broadcasted_iota(jnp.int32, (TILE, 1), 0).astype(jnp.float32) + float(h)
    for c in range(0, cols, 2):
        sides = []
        for d in (c, c + 1):
            mine = back[d * h : (d + 1) * h]
            sides.append(jnp.concatenate([mine[:, :n], mine[:, n:]], axis=0))
        corr = jnp.dot(last, jnp.concatenate(sides, axis=1), preferred_element_type=jnp.float32)
        power = corr * corr
        total = power[:TILE]
        ramp = total
        for t in range(1, n // TILE):
            total = total + power[t * TILE : (t + 1) * TILE]
            ramp = ramp + total
        shifted = place * total - float(TILE) * ramp
        total = jnp.sum(total, axis=0, keepdims=True)
        shifted = jnp.sum(shifted, axis=0, keepdims=True)
        for d in (0, 1):
            sums[c + d : c + d + 1, :] = shifted[:, d * n : (d + 1) * n]
            sums[cols + c + d : cols + c + d + 1, :] = total[:, d * n : (d + 1) * n]
    return lax.dot_general(
        weigh,
        sums[...],
        (((1,), (1,)), ((), ())),
        precision=lax.Precision.HIGHEST,
        preferred_element_type=jnp.float32,
    )


def own_kernel(reach, x, first, second, inverse, last, weigh, red, tail, spec, sums):
    row = pl.program_id(0)
    step = pl.program_id(1)
    local = pl.num_programs(1)
    cols, n = x.shape[2], x.shape[-1]

    def put(c, value):
        spec[step, c] = value

    spectra(x[0, 0], first[...], second[...], put)

    @pl.when(step >= local - reach)
    def _():
        tail[jnp.maximum(step - (local - reach), 0), 0] = spec[step].astype(tail.dtype)

    def body(offset, carry):
        red[step - offset, offset - 1, row] = pairs(
            lambda c: spec[step - offset, c],
            lambda c: spec[step, c],
            cols, n, inverse[...], last[...], weigh[...], sums,
        )
        return carry

    lax.fori_loop(1, jnp.minimum(step, reach) + 1, body, 0)


def far_kernel(count, x, first, second, inverse, last, weigh, *rest):
    own, red, spec, sums = rest[:count], rest[count], rest[count + 1], rest[count + 2]
    cols, n = x.shape[2], x.shape[-1]

    def put(c, value):
        spec[c] = value

    spectra(x[0, 0], first[...], second[...], put)
    for item in range(count):
        red[item, 0] = pairs(
            lambda c: own[item][0, 0, c].astype(jnp.float32),
            lambda c: spec[c],
            cols, n, inverse[...], last[...], weigh[...], sums,
        )


def fixed(array):
    zeros = (0,) * array.ndim
    return pl.BlockSpec(array.shape, lambda *_: zeros)


def cost(patches, pair_count, n):
    return pl.CostEstimate(
        flops=(patches + pair_count) * 24 * n**3,
        bytes_accessed=patches * n * n * 16,
        transcendentals=0,
    )


def relax_kernel(sizes, base, out, slots, field, weight, send, recv):
    groups, tiles, local, reach, span, grid_rows, grid_cols = sizes
    half = LANES // 2
    sec = lax.axis_index("sec")
    tile = lax.axis_index("tile")
    me = sec * tiles + tile
    count = groups * tiles

    def place(index):
        return (index // tiles, index % tiles)

    barrier = pltpu.get_barrier_semaphore()

    def greet(d, carry):
        pl.semaphore_signal(
            barrier, inc=1, device_id=place((me + d) % count), device_id_type=MESH
        )
        return carry

    lax.fori_loop(1, count, greet, 0)
    pl.semaphore_wait(barrier, count - 1)

    def copy(slot, peer):
        return pltpu.make_async_remote_copy(
            src_ref=base,
            dst_ref=slots.at[slot],
            send_sem=send.at[peer],
            recv_sem=recv.at[slot],
            device_id=place(peer),
            device_id_type=MESH,
        )

    def start(d, carry):
        copy(me, (me + d) % count).start()
        return carry

    lax.fori_loop(1, count, start, 0)
    slots[me] = base[...]

    def finish(d, carry):
        peer = (me + d) % count
        copy(peer, peer).wait_recv()
        copy(me, peer).wait_send()
        return carry

    lax.fori_loop(1, count, finish, 0)

    lane = lax.broadcasted_iota(jnp.int32, (TILE, LANES), 1)
    sub = lax.broadcasted_iota(jnp.int32, (TILE, LANES), 0)
    owner = lane % half // span
    for g in range(groups):
        blocks = [slots[g * tiles + t] for t in range(tiles)]
        for v in range(reach + 1):
            value = jnp.zeros((TILE, LANES), jnp.float32)
            for t in range(tiles):
                moved = blocks[t]
                if t != v:
                    moved = pltpu.roll(moved, (t - v) * span % LANES, 1)
                value = jnp.where(owner == t, moved, value)
            field[v, g * local : (g + 1) * local, :] = value[:local]
        row = jnp.broadcast_to(blocks[0][local : local + 1], (TILE, LANES))
        for v in range(reach):
            w = jnp.sum(jnp.where(lane == sub * reach + v, row, 0.0), axis=1, keepdims=True)
            w = jnp.broadcast_to(w, (TILE, LANES))
            weight[v, g * local : (g + 1) * local, :] = w[:local]

    total = groups * local
    spot = lax.broadcasted_iota(jnp.int32, (total, LANES), 1) % half
    across = spot % grid_cols
    down = spot // grid_cols
    one = lambda mask: mask.astype(jnp.float32)
    left, right = one(across > 0), one(across < grid_cols - 1)
    up, below = one(down > 0), one(down < grid_rows - 1)

    def sweep(_, u):
        plane = (
            up * (pltpu.roll(u, grid_cols, 1) - u)
            + below * (pltpu.roll(u, LANES - grid_cols, 1) - u)
            + left * (pltpu.roll(u, 1, 1) - u)
            + right * (pltpu.roll(u, LANES - 1, 1) - u)
        )
        spring = jnp.zeros_like(u)
        for v in range(reach):
            o = v + 1
            r = weight[v] * (pltpu.roll(u, total - o, 0) - u - field[v])
            spring = spring + r - pltpu.roll(r, o, 0)
        return u + STEP_SIZE * (plane + spring)

    state = lax.fori_loop(0, SWEEPS, sweep, field[reach])
    field[reach] = state
    mine = field[reach, pl.ds(sec * local, local), :]
    mine = jnp.concatenate([mine, jnp.zeros((TILE - local, LANES), jnp.float32)], axis=0)
    out[...] = pltpu.roll(mine, (LANES - tile * span) % LANES, 1)


def shards(patches, pair_flags, nodes):
    local, rows, cols, n = patches.shape[:4]
    reach = pair_flags.shape[1]
    groups, tiles = lax.axis_size("sec"), lax.axis_size("tile")
    part = n // 2 + TILE
    tabs = [jnp.asarray(t) for t in tables(n)]
    tab_specs = [fixed(t) for t in tabs]
    back_by_one = [(i, i - 1) for i in range(1, groups)]
    ahead = [lax.ppermute(patches[r : r + 1], "sec", back_by_one) for r in range(reach)]

    patch_block = (1, 1, cols, n, n)
    red, tail = pl.pallas_call(
        functools.partial(own_kernel, reach),
        grid=(rows, local),
        in_specs=[pl.BlockSpec(patch_block, lambda i, s: (s, i, 0, 0, 0))] + tab_specs,
        out_specs=[
            pl.BlockSpec((local, reach, rows, TILE, 2 * cols), lambda i, s: (0, 0, 0, 0, 0)),
            pl.BlockSpec((reach, 1, cols, 2 * part, n), lambda i, s: (0, i, 0, 0, 0)),
        ],
        out_shape=[
            jax.ShapeDtypeStruct((local, reach, rows, TILE, 2 * cols), jnp.float32),
            jax.ShapeDtypeStruct((reach, rows, cols, 2 * part, n), jnp.bfloat16),
        ],
        scratch_shapes=[
            pltpu.VMEM((local, cols, 2 * part, n), jnp.float32),
            pltpu.VMEM((2 * cols, n), jnp.float32),
        ],
        compiler_params=pltpu.CompilerParams(
            dimension_semantics=("arbitrary", "arbitrary"), vmem_limit_bytes=40 << 20
        ),
        cost_estimate=cost(local * rows * cols, (reach * local - reach * (reach + 1) // 2) * rows * cols, n),
        name="own_pairs",
    )(patches, *tabs)

    grid = {}
    for r in range(reach):
        count = reach - r
        own_specs = [
            pl.BlockSpec((1, 1, cols, 2 * part, n), functools.partial(lambda k, i: (k, i, 0, 0, 0), k))
            for k in range(r, reach)
        ]
        far = pl.pallas_call(
            functools.partial(far_kernel, count),
            grid=(rows,),
            in_specs=[pl.BlockSpec(patch_block, lambda i: (0, i, 0, 0, 0))] + tab_specs + own_specs,
            out_specs=pl.BlockSpec((count, 1, TILE, 2 * cols), lambda i: (0, i, 0, 0)),
            out_shape=jax.ShapeDtypeStruct((count, rows, TILE, 2 * cols), jnp.float32),
            scratch_shapes=[
                pltpu.VMEM((cols, 2 * part, n), jnp.float32),
                pltpu.VMEM((2 * cols, n), jnp.float32),
            ],
            compiler_params=pltpu.CompilerParams(
                dimension_semantics=("arbitrary",), vmem_limit_bytes=24 << 20
            ),
            cost_estimate=cost(rows * cols, count * rows * cols, n),
            name=f"far_pairs_{r}",
        )(ahead[r], *tabs, *([tail] * count))
        for item in range(count):
            section = local - reach + r + item
            grid[section, local + r - section] = far[item]
    stats = jnp.stack(
        [
            jnp.stack([grid.get((s, o), red[s, o - 1]) for o in range(1, reach + 1)], 0)
            for s in range(local)
        ],
        0,
    )

    placed = lax.axis_index("sec") * local + jnp.arange(local, dtype=jnp.int32)
    offsets = jnp.arange(1, reach + 1, dtype=jnp.int32)
    weights = pair_flags.astype(jnp.float32) * (
        placed[:, None] + offsets[None, :] < groups * local
    ).astype(jnp.float32)
    area = float(n * n)
    total = stats[..., 0, cols:] / area + EPSILON
    ratio = jnp.stack([stats[..., 0, :cols], stats[..., 1, cols:]], 0) / area / total
    measured = ratio * weights[None, :, :, None, None]

    span = rows * cols
    lanes = jnp.concatenate(
        [
            jnp.transpose(measured, (1, 0, 2, 3, 4)).reshape(local, 2, reach * span),
            jnp.transpose(nodes, (1, 0, 2, 3)).reshape(local, 2, span),
        ],
        axis=2,
    )
    lanes = jnp.pad(lanes, ((0, 0), (0, 0), (0, LANES // 2 - (reach + 1) * span)))
    flat = jnp.pad(weights.reshape(1, local * reach), ((0, 0), (0, LANES - local * reach)))
    base = jnp.concatenate([lanes.reshape(local, LANES), flat], axis=0)
    base = jnp.pad(base, ((0, TILE - local - 1), (0, 0)))

    sizes = (groups, tiles, local, reach, span, tiles * rows, cols)
    vmem = pl.BlockSpec(memory_space=pltpu.VMEM)
    moved = pl.pallas_call(
        functools.partial(relax_kernel, sizes),
        in_specs=[vmem],
        out_specs=vmem,
        out_shape=jax.ShapeDtypeStruct((TILE, LANES), jnp.float32),
        scratch_shapes=[
            pltpu.VMEM((groups * tiles, TILE, LANES), jnp.float32),
            pltpu.VMEM((reach + 1, groups * local, LANES), jnp.float32),
            pltpu.VMEM((reach, groups * local, LANES), jnp.float32),
            pltpu.SemaphoreType.DMA((groups * tiles,)),
            pltpu.SemaphoreType.DMA((groups * tiles,)),
        ],
        compiler_params=pltpu.CompilerParams(
            collective_id=0, has_side_effects=True, vmem_limit_bytes=24 << 20
        ),
        name="relax",
    )(base)
    positions = moved[:local].reshape(local, 2, LANES // 2)[:, :, :span]
    positions = jnp.transpose(positions.reshape(local, 2, rows, cols), (1, 0, 2, 3))
    return (positions, measured)


def solution(mesh):
    placed = (P("sec", "tile", None, None, None), P("sec", None), P(None, "sec", "tile", None))
    return jax.shard_map(
        shards,
        mesh=mesh,
        in_specs=placed,
        out_specs=(P(None, "sec", "tile", None), P(None, "sec", None, "tile", None)),
        check_vma=False,
    )
```

```python
import functools
import math

import jax
import jax.numpy as jnp
import numpy as np
from jax import lax
from jax.experimental import pallas as pl
from jax.experimental.pallas import tpu as pltpu
from jax.sharding import PartitionSpec as P


SWEEPS = 8
STEP_SIZE = 0.08
EPSILON = 1e-06
LANES = 128
TILE = 8
MESH = pl.DeviceIdType.MESH


def tables(n):
    h = n // 2
    k = np.arange(n)
    phase = (k[:, None] * k[None, :] % n) * (2.0 * math.pi / n)
    c = np.asarray(np.cos(phase), np.float32).astype(jnp.bfloat16).astype(np.float32)
    s = np.asarray(np.sin(phase), np.float32).astype(jnp.bfloat16).astype(np.float32)
    part = h + TILE
    first = np.zeros((2 * part, 2 * n), np.float32)
    first[: h + 1, :n] = c[: h + 1]
    first[part : part + h, :n] = s[:h]
    second = np.concatenate([np.concatenate([c, -s], 1), np.concatenate([-s, -c], 1)], 0)
    inverse = np.concatenate([np.concatenate([c, s], 1), np.concatenate([-s, c], 1)], 0)
    order = (np.arange(n) - h) % n
    last = np.zeros((n, 2 * n), np.float32)
    last[:, 0] = c[order, 0]
    last[:, 1:h] = 2.0 * c[order, 1:h]
    last[:, h] = c[order, h]
    last[:, h + 1 : n] = -2.0 * s[order, 1:h]
    last *= 1.0 / float(n) ** 3
    return np.concatenate([first, second, inverse, last], 0).astype(jnp.bfloat16)


def open_tables(tab, n):
    part = n // 2 + TILE
    first = tab[: 2 * part, :n]
    second = tab[2 * part : 2 * part + 2 * n]
    inverse = tab[2 * part + 2 * n : 2 * part + 4 * n]
    last = tab[2 * part + 4 * n :, :n]
    sub = lax.broadcasted_iota(jnp.int32, (TILE, n), 0)
    lane = lax.broadcasted_iota(jnp.int32, (TILE, n), 1)
    shift = jnp.where(lane < n // 2, lane, lane - n).astype(jnp.float32)
    weigh = jnp.where(sub == 0, 1.0, jnp.where(sub == 1, shift, 0.0))
    return (first, second), (inverse, last, weigh)


def spectra(x, first, second, put):
    cols, n = x.shape[0], x.shape[-1]
    part = n // 2 + TILE
    lines = []
    for c in range(0, cols, 2):
        y = jnp.dot(
            first, jnp.concatenate([x[c], x[c + 1]], axis=1), preferred_element_type=jnp.float32
        )
        for d in (0, 1):
            mine = y[:, d * n : (d + 1) * n]
            lines.append(jnp.concatenate([mine[:part], mine[part:]], axis=1))
    lines = jnp.concatenate(lines, axis=0).astype(jnp.bfloat16)
    spec = jnp.dot(lines, second, preferred_element_type=jnp.float32)
    for c in range(cols):
        mine = spec[c * part : (c + 1) * part]
        put(c, mine[:, :n], mine[:, n:])


def pairs(get_a, get_b, cols, n, inverse, last, weigh, sums):
    h = n // 2
    part = h + TILE
    crosses = []
    for c in range(cols):
        a, b = get_a(c), get_b(c)
        ar, ai, br, bi = a[:part], a[part:], b[:part], b[part:]
        real = ar * br + ai * bi
        imag = ar * bi - ai * br
        real_top = real[:TILE] - imag[h:]
        imag_top = imag[:TILE] + real[h:]
        real = jnp.concatenate([real_top, real[TILE:h]], axis=0).astype(jnp.bfloat16)
        imag = jnp.concatenate([imag_top, imag[TILE:h]], axis=0).astype(jnp.bfloat16)
        crosses.append(jnp.concatenate([real, imag], axis=1))
    back = jnp.dot(
        jnp.concatenate(crosses, axis=0), inverse, preferred_element_type=jnp.float32
    ).astype(jnp.bfloat16)
    place = lax.broadcasted_iota(jnp.int32, (TILE, 1), 0).astype(jnp.float32) + float(h)
    for c in range(0, cols, 2):
        sides = []
        for d in (c, c + 1):
            mine = back[d * h : (d + 1) * h]
            sides.append(jnp.concatenate([mine[:, :n], mine[:, n:]], axis=0))
        corr = jnp.dot(last, jnp.concatenate(sides, axis=1), preferred_element_type=jnp.float32)
        power = corr * corr
        total = power[:TILE]
        ramp = total
        for t in range(1, n // TILE):
            total = total + power[t * TILE : (t + 1) * TILE]
            ramp = ramp + total
        shifted = place * total - float(TILE) * ramp
        total = jnp.sum(total, axis=0, keepdims=True)
        shifted = jnp.sum(shifted, axis=0, keepdims=True)
        for d in (0, 1):
            sums[c + d : c + d + 1, :] = shifted[:, d * n : (d + 1) * n]
            sums[cols + c + d : cols + c + d + 1, :] = total[:, d * n : (d + 1) * n]
    return lax.dot_general(
        weigh,
        sums[...],
        (((1,), (1,)), ((), ())),
        precision=lax.Precision.HIGHEST,
        preferred_element_type=jnp.float32,
    )


def own_kernel(reach, x, tab, red, tail, spec, sums):
    row = pl.program_id(0)
    step = pl.program_id(1)
    local = pl.num_programs(1)
    cols, n = x.shape[2], x.shape[-1]

    part = n // 2 + TILE
    forward, inverse = open_tables(tab, n)

    def put(c, real, imag):
        spec[step, c, :part] = real
        spec[step, c, part:] = imag

    spectra(x.at[0, 0], *forward, put)

    @pl.when(step >= local - reach)
    def _():
        tail[jnp.maximum(step - (local - reach), 0), 0] = spec[step].astype(tail.dtype)

    def body(offset, carry):
        red[step - offset, offset - 1, row] = pairs(
            lambda c: spec[step - offset, c],
            lambda c: spec[step, c],
            cols, n, *inverse, sums,
        )
        return carry

    lax.fori_loop(1, jnp.minimum(step, reach) + 1, body, 0)


def far_kernel(count, x, tab, *rest):
    own, red, spec, sums = rest[:count], rest[count], rest[count + 1], rest[count + 2]
    cols, n = x.shape[2], x.shape[-1]

    part = n // 2 + TILE
    forward, inverse = open_tables(tab, n)

    def put(c, real, imag):
        spec[c, :part] = real
        spec[c, part:] = imag

    spectra(x.at[0, 0], *forward, put)
    for item in range(count):
        red[item, 0] = pairs(
            lambda c: own[item][0, 0, c].astype(jnp.float32),
            lambda c: spec[c],
            cols, n, *inverse, sums,
        )


def fixed(array):
    zeros = (0,) * array.ndim
    return pl.BlockSpec(array.shape, lambda *_: zeros)


def cost(patches, pair_count, n):
    return pl.CostEstimate(
        flops=(patches + pair_count) * 24 * n**3,
        bytes_accessed=patches * n * n * 16,
        transcendentals=0,
    )


def relax_kernel(sizes, base, out, slots, field, weight, send, recv):
    groups, tiles, local, reach, span, grid_rows, grid_cols = sizes
    half = LANES // 2
    sec = lax.axis_index("sec")
    tile = lax.axis_index("tile")
    me = sec * tiles + tile
    count = groups * tiles
    unroll = count <= 64

    def place(index):
        return (index // tiles, index % tiles)

    barrier = pltpu.get_barrier_semaphore()

    def greet(d, carry):
        pl.semaphore_signal(
            barrier, inc=1, device_id=place((me + d) % count), device_id_type=MESH
        )
        return carry

    lax.fori_loop(1, count, greet, 0, unroll=unroll)
    pl.semaphore_wait(barrier, count - 1)

    def copy(slot, peer):
        return pltpu.make_async_remote_copy(
            src_ref=base,
            dst_ref=slots.at[slot],
            send_sem=send.at[peer],
            recv_sem=recv.at[slot],
            device_id=place(peer),
            device_id_type=MESH,
        )

    def start(d, carry):
        copy(me, (me + d) % count).start()
        return carry

    lax.fori_loop(1, count, start, 0, unroll=unroll)
    slots[me] = base[...]

    def finish(d, carry):
        peer = (me + d) % count
        copy(peer, peer).wait_recv()
        copy(me, peer).wait_send()
        return carry

    lax.fori_loop(1, count, finish, 0, unroll=unroll)

    lane = lax.broadcasted_iota(jnp.int32, (TILE, LANES), 1)
    sub = lax.broadcasted_iota(jnp.int32, (TILE, LANES), 0)
    owner = lane % half // span
    for g in range(groups):
        blocks = [slots[g * tiles + t] for t in range(tiles)]
        for v in range(reach + 1):
            value = jnp.zeros((TILE, LANES), jnp.float32)
            for t in range(tiles):
                moved = blocks[t]
                if t != v:
                    moved = pltpu.roll(moved, (t - v) * span % LANES, 1)
                value = jnp.where(owner == t, moved, value)
            field[v, g * local : (g + 1) * local, :] = value[:local]
        row = jnp.broadcast_to(blocks[0][local : local + 1], (TILE, LANES))
        for v in range(reach):
            w = jnp.sum(jnp.where(lane == sub * reach + v, row, 0.0), axis=1, keepdims=True)
            w = jnp.broadcast_to(w, (TILE, LANES))
            weight[v, g * local : (g + 1) * local, :] = w[:local]

    total = groups * local
    spot = lax.broadcasted_iota(jnp.int32, (total, LANES), 1) % half
    across = spot % grid_cols
    down = spot // grid_cols
    one = lambda mask: mask.astype(jnp.float32)
    left, right = one(across > 0), one(across < grid_cols - 1)
    up, below = one(down > 0), one(down < grid_rows - 1)

    def sweep(_, u):
        plane = (
            up * (pltpu.roll(u, grid_cols, 1) - u)
            + below * (pltpu.roll(u, LANES - grid_cols, 1) - u)
            + left * (pltpu.roll(u, 1, 1) - u)
            + right * (pltpu.roll(u, LANES - 1, 1) - u)
        )
        spring = jnp.zeros_like(u)
        for v in range(reach):
            o = v + 1
            r = weight[v] * (pltpu.roll(u, total - o, 0) - u - field[v])
            spring = spring + r - pltpu.roll(r, o, 0)
        return u + STEP_SIZE * (plane + spring)

    state = lax.fori_loop(0, SWEEPS, sweep, field[reach])
    field[reach] = state
    mine = field[reach, pl.ds(sec * local, local), :]
    mine = jnp.concatenate([mine, jnp.zeros((TILE - local, LANES), jnp.float32)], axis=0)
    out[...] = pltpu.roll(mine, (LANES - tile * span) % LANES, 1)


def shards(patches, pair_flags, nodes):
    local, rows, cols, n = patches.shape[:4]
    reach = pair_flags.shape[1]
    groups, tiles = lax.axis_size("sec"), lax.axis_size("tile")
    part = n // 2 + TILE
    tab = jnp.asarray(tables(n))
    back_by_one = [(i, i - 1) for i in range(1, groups)]
    head = patches[: reach - 1]
    early = lax.ppermute(head, "sec", back_by_one)
    _, rest = lax.optimization_barrier((head, patches))
    late = lax.ppermute(rest[reach - 1 : reach], "sec", back_by_one)

    patch_block = (1, 1, cols, n, n)
    red, tail = pl.pallas_call(
        functools.partial(own_kernel, reach),
        grid=(rows, local),
        in_specs=[pl.BlockSpec(patch_block, lambda i, s: (s, i, 0, 0, 0))] + [fixed(tab)],
        out_specs=[
            pl.BlockSpec((local, reach, rows, TILE, 2 * cols), lambda i, s: (0, 0, 0, 0, 0)),
            pl.BlockSpec((reach, 1, cols, 2 * part, n), lambda i, s: (0, i, 0, 0, 0)),
        ],
        out_shape=[
            jax.ShapeDtypeStruct((local, reach, rows, TILE, 2 * cols), jnp.float32),
            jax.ShapeDtypeStruct((reach, rows, cols, 2 * part, n), jnp.bfloat16),
        ],
        scratch_shapes=[
            pltpu.VMEM((local, cols, 2 * part, n), jnp.float32),
            pltpu.VMEM((2 * cols, n), jnp.float32),
        ],
        compiler_params=pltpu.CompilerParams(
            dimension_semantics=("arbitrary", "arbitrary"), vmem_limit_bytes=40 << 20
        ),
        cost_estimate=cost(local * rows * cols, (reach * local - reach * (reach + 1) // 2) * rows * cols, n),
        name="own_pairs",
    )(patches, tab)

    grid = {}
    for r in range(reach):
        count = reach - r
        received, spot = (early, r) if r < reach - 1 else (late, 0)
        own_specs = [
            pl.BlockSpec((1, 1, cols, 2 * part, n), functools.partial(lambda k, i: (k, i, 0, 0, 0), k))
            for k in range(r, reach)
        ]
        far_call = pl.pallas_call(
            functools.partial(far_kernel, count),
            grid=(rows,),
            in_specs=[pl.BlockSpec(patch_block, functools.partial(lambda k, i: (k, i, 0, 0, 0), spot))] + [fixed(tab)] + own_specs,
            out_specs=pl.BlockSpec((count, 1, TILE, 2 * cols), lambda i: (0, i, 0, 0)),
            out_shape=jax.ShapeDtypeStruct((count, rows, TILE, 2 * cols), jnp.float32),
            scratch_shapes=[
                pltpu.VMEM((cols, 2 * part, n), jnp.float32),
                pltpu.VMEM((2 * cols, n), jnp.float32),
            ],
            compiler_params=pltpu.CompilerParams(
                dimension_semantics=("arbitrary",), vmem_limit_bytes=24 << 20
            ),
            cost_estimate=cost(rows * cols, count * rows * cols, n),
        )
        far = far_call(received, tab, *([tail] * count))
        for item in range(count):
            section = local - reach + r + item
            grid[section, local + r - section] = far[item]
    stats = jnp.stack(
        [
            jnp.stack([grid.get((s, o), red[s, o - 1]) for o in range(1, reach + 1)], 0)
            for s in range(local)
        ],
        0,
    )

    placed = lax.axis_index("sec") * local + jnp.arange(local, dtype=jnp.int32)
    offsets = jnp.arange(1, reach + 1, dtype=jnp.int32)
    weights = pair_flags.astype(jnp.float32) * (
        placed[:, None] + offsets[None, :] < groups * local
    ).astype(jnp.float32)
    area = float(n * n)
    total = stats[..., 0, cols:] / area + EPSILON
    ratio = jnp.stack([stats[..., 0, :cols], stats[..., 1, cols:]], 0) / area / total
    measured = ratio * weights[None, :, :, None, None]

    span = rows * cols
    lanes = jnp.concatenate(
        [
            jnp.transpose(measured, (1, 0, 2, 3, 4)).reshape(local, 2, reach * span),
            jnp.transpose(nodes, (1, 0, 2, 3)).reshape(local, 2, span),
        ],
        axis=2,
    )
    lanes = jnp.pad(lanes, ((0, 0), (0, 0), (0, LANES // 2 - (reach + 1) * span)))
    flat = jnp.pad(weights.reshape(1, local * reach), ((0, 0), (0, LANES - local * reach)))
    base = jnp.concatenate([lanes.reshape(local, LANES), flat], axis=0)
    base = jnp.pad(base, ((0, TILE - local - 1), (0, 0)))

    sizes = (groups, tiles, local, reach, span, tiles * rows, cols)
    vmem = pl.BlockSpec(memory_space=pltpu.VMEM)
    moved = pl.pallas_call(
        functools.partial(relax_kernel, sizes),
        in_specs=[vmem],
        out_specs=vmem,
        out_shape=jax.ShapeDtypeStruct((TILE, LANES), jnp.float32),
        scratch_shapes=[
            pltpu.VMEM((groups * tiles, TILE, LANES), jnp.float32),
            pltpu.VMEM((reach + 1, groups * local, LANES), jnp.float32),
            pltpu.VMEM((reach, groups * local, LANES), jnp.float32),
            pltpu.SemaphoreType.DMA((groups * tiles,)),
            pltpu.SemaphoreType.DMA((groups * tiles,)),
        ],
        compiler_params=pltpu.CompilerParams(
            collective_id=0, has_side_effects=True, vmem_limit_bytes=24 << 20
        ),
        name="relax",
    )(base)
    positions = moved[:local].reshape(local, 2, LANES // 2)[:, :, :span]
    positions = jnp.transpose(positions.reshape(local, 2, rows, cols), (1, 0, 2, 3))
    return (positions, measured)


def solution(mesh):
    placed = (P("sec", "tile", None, None, None), P("sec", None), P(None, "sec", "tile", None))
    return jax.shard_map(
        shards,
        mesh=mesh,
        in_specs=placed,
        out_specs=(P(None, "sec", "tile", None), P(None, "sec", None, "tile", None)),
        check_vma=False,
    )
```

```python
import functools
import math

import jax
import jax.numpy as jnp
import numpy as np
from jax import lax
from jax.experimental import pallas as pl
from jax.experimental.pallas import tpu as pltpu
from jax.sharding import PartitionSpec as P


SWEEPS = 8
STEP_SIZE = 0.08
EPSILON = 1e-06
LANES = 128
TILE = 8
MESH = pl.DeviceIdType.MESH


def tables(n):
    h = n // 2
    k = np.arange(n)
    phase = (k[:, None] * k[None, :] % n) * (2.0 * math.pi / n)
    c = np.asarray(np.cos(phase), np.float32).astype(jnp.bfloat16).astype(np.float32)
    s = np.asarray(np.sin(phase), np.float32).astype(jnp.bfloat16).astype(np.float32)
    part = h + TILE
    first = np.zeros((2 * part, 2 * n), np.float32)
    first[: h + 1, :n] = c[: h + 1]
    first[part : part + h, :n] = s[:h]
    second = np.concatenate([np.concatenate([c, -s], 1), np.concatenate([-s, -c], 1)], 0)
    inverse = np.concatenate([np.concatenate([c, s], 1), np.concatenate([-s, c], 1)], 0)
    order = (np.arange(n) - h) % n
    last = np.zeros((n, 2 * n), np.float32)
    last[:, 0] = c[order, 0]
    last[:, 1:h] = 2.0 * c[order, 1:h]
    last[:, h] = c[order, h]
    last[:, h + 1 : n] = -2.0 * s[order, 1:h]
    last *= 1.0 / float(n) ** 3
    return np.concatenate([first, second, inverse, last], 0).astype(jnp.bfloat16)


def open_tables(tab, n):
    part = n // 2 + TILE
    first = tab[: 2 * part, :n]
    second = tab[2 * part : 2 * part + 2 * n]
    inverse = tab[2 * part + 2 * n : 2 * part + 4 * n]
    last = tab[2 * part + 4 * n :, :n]
    sub = lax.broadcasted_iota(jnp.int32, (TILE, n), 0)
    lane = lax.broadcasted_iota(jnp.int32, (TILE, n), 1)
    shift = jnp.where(lane < n // 2, lane, lane - n).astype(jnp.float32)
    weigh = jnp.where(sub == 0, 1.0, jnp.where(sub == 1, shift, 0.0))
    return (first, second), (inverse, last, weigh)


def spectra(x, first, second, put):
    cols, n = x.shape[0], x.shape[-1]
    part = n // 2 + TILE
    lines = []
    for c in range(0, cols, 2):
        y = jnp.dot(
            first, jnp.concatenate([x[c], x[c + 1]], axis=1), preferred_element_type=jnp.float32
        )
        for d in (0, 1):
            mine = y[:, d * n : (d + 1) * n]
            lines.append(jnp.concatenate([mine[:part], mine[part:]], axis=1))
    lines = jnp.concatenate(lines, axis=0).astype(jnp.bfloat16)
    spec = jnp.dot(lines, second, preferred_element_type=jnp.float32)
    for c in range(cols):
        mine = spec[c * part : (c + 1) * part]
        put(c, mine[:, :n], mine[:, n:])


def pairs(get_a, get_b, cols, n, inverse, last, weigh, sums):
    h = n // 2
    part = h + TILE
    crosses = []
    for c in range(cols):
        a, b = get_a(c), get_b(c)
        ar, ai, br, bi = a[:part], a[part:], b[:part], b[part:]
        real = ar * br + ai * bi
        imag = ar * bi - ai * br
        real_top = real[:TILE] - imag[h:]
        imag_top = imag[:TILE] + real[h:]
        real = jnp.concatenate([real_top, real[TILE:h]], axis=0).astype(jnp.bfloat16)
        imag = jnp.concatenate([imag_top, imag[TILE:h]], axis=0).astype(jnp.bfloat16)
        crosses.append(jnp.concatenate([real, imag], axis=1))
    back = jnp.dot(
        jnp.concatenate(crosses, axis=0), inverse, preferred_element_type=jnp.float32
    ).astype(jnp.bfloat16)
    place = lax.broadcasted_iota(jnp.int32, (TILE, 1), 0).astype(jnp.float32) + float(h)
    for c in range(0, cols, 2):
        sides = []
        for d in (c, c + 1):
            mine = back[d * h : (d + 1) * h]
            sides.append(jnp.concatenate([mine[:, :n], mine[:, n:]], axis=0))
        corr = jnp.dot(last, jnp.concatenate(sides, axis=1), preferred_element_type=jnp.float32)
        power = corr * corr
        total = power[:TILE]
        ramp = total
        for t in range(1, n // TILE):
            total = total + power[t * TILE : (t + 1) * TILE]
            ramp = ramp + total
        shifted = place * total - float(TILE) * ramp
        total = jnp.sum(total, axis=0, keepdims=True)
        shifted = jnp.sum(shifted, axis=0, keepdims=True)
        for d in (0, 1):
            sums[c + d : c + d + 1, :] = shifted[:, d * n : (d + 1) * n]
            sums[cols + c + d : cols + c + d + 1, :] = total[:, d * n : (d + 1) * n]
    return lax.dot_general(
        weigh,
        sums[...],
        (((1,), (1,)), ((), ())),
        precision=lax.Precision.HIGHEST,
        preferred_element_type=jnp.float32,
    )


def own_kernel(reach, x, tab, red, tail, edge, spec, sums):
    step = pl.program_id(0)
    local = pl.num_programs(0)
    rows, cols, n = x.shape[1], x.shape[2], x.shape[-1]

    part = n // 2 + TILE
    forward, inverse = open_tables(tab, n)

    for row in range(rows):

        def put(c, real, imag):
            spec[step, row, c, :part] = real
            spec[step, row, c, part:] = imag

        spectra(x.at[0, row], *forward, put)

    @pl.when(step >= local - reach)
    def _():
        tail[jnp.maximum(step - (local - reach), 0)] = spec[step].astype(tail.dtype)

    @pl.when(step == local - 1)
    def _():
        edge[0] = spec[step].astype(edge.dtype)

    def body(offset, carry):
        for row in range(rows):
            red[step - offset, offset - 1, row] = pairs(
                lambda c: spec[step - offset, row, c],
                lambda c: spec[step, row, c],
                cols, n, *inverse, sums.at[row],
            )
        return carry

    lax.fori_loop(1, jnp.minimum(step, reach) + 1, body, 0)


def far_kernel(count, x, tab, *rest):
    own, red, spec, sums = rest[:count], rest[count], rest[count + 1], rest[count + 2]
    cols, n = x.shape[2], x.shape[-1]

    part = n // 2 + TILE
    forward, inverse = open_tables(tab, n)

    def put(c, real, imag):
        spec[c, :part] = real
        spec[c, part:] = imag

    spectra(x.at[0, 0], *forward, put)
    for item in range(count):
        red[item, 0] = pairs(
            lambda c: own[item][0, 0, c].astype(jnp.float32),
            lambda c: spec[c],
            cols, n, *inverse, sums,
        )


def fixed(array):
    zeros = (0,) * array.ndim
    return pl.BlockSpec(array.shape, lambda *_: zeros)


def cost(patches, pair_count, n):
    return pl.CostEstimate(
        flops=(patches + pair_count) * 24 * n**3,
        bytes_accessed=patches * n * n * 16,
        transcendentals=0,
    )


def relax_kernel(
    sizes, base, late, tab, tail, out, payload, slots, field, weight, spec, sums, send, recv
):
    groups, tiles, local, reach, span, grid_rows, grid_cols = sizes
    half = LANES // 2
    sec = lax.axis_index("sec")
    tile = lax.axis_index("tile")
    me = sec * tiles + tile
    count = groups * tiles
    unroll = count <= 64

    def place(index):
        return (index // tiles, index % tiles)

    barrier = pltpu.get_barrier_semaphore()

    def greet(d, carry):
        pl.semaphore_signal(
            barrier, inc=1, device_id=place((me + d) % count), device_id_type=MESH
        )
        return carry

    lax.fori_loop(1, count, greet, 0, unroll=unroll)

    rows, cols, n = late.shape[1], late.shape[2], late.shape[-1]
    part = n // 2 + TILE
    forward, inverse = open_tables(tab, n)
    for row in range(rows):

        def put(c, real, imag):
            spec[row, c, :part] = real
            spec[row, c, part:] = imag

        spectra(late.at[0, row], *forward, put)
    payload[...] = base[...]
    key = (local - 1) * reach + reach - 1
    flag = base[local : local + 1, key : key + 1]
    for row in range(rows):
        red = pairs(
            lambda c: tail[0, row, c].astype(jnp.float32),
            lambda c: spec[row, c],
            cols, n, *inverse, sums.at[row],
        )
        area = float(n * n)
        scale = flag / (red[:1, cols:] / area + EPSILON)
        at = (reach - 1) * span + row * cols
        payload[local - 1 : local, at : at + cols] = red[:1, :cols] / area * scale
        payload[local - 1 : local, half + at : half + at + cols] = red[1:2, cols:] / area * scale
    pl.semaphore_wait(barrier, count - 1)

    def copy(slot, peer):
        return pltpu.make_async_remote_copy(
            src_ref=payload,
            dst_ref=slots.at[slot],
            send_sem=send.at[peer],
            recv_sem=recv.at[slot],
            device_id=place(peer),
            device_id_type=MESH,
        )

    def start(d, carry):
        copy(me, (me + d) % count).start()
        return carry

    lax.fori_loop(1, count, start, 0, unroll=unroll)
    slots[me] = payload[...]

    def finish(d, carry):
        peer = (me + d) % count
        copy(peer, peer).wait_recv()
        copy(me, peer).wait_send()
        return carry

    lax.fori_loop(1, count, finish, 0, unroll=unroll)

    lane = lax.broadcasted_iota(jnp.int32, (TILE, LANES), 1)
    sub = lax.broadcasted_iota(jnp.int32, (TILE, LANES), 0)
    owner = lane % half // span
    for g in range(groups):
        blocks = [slots[g * tiles + t] for t in range(tiles)]
        for v in range(reach + 1):
            value = jnp.zeros((TILE, LANES), jnp.float32)
            for t in range(tiles):
                moved = blocks[t]
                if t != v:
                    moved = pltpu.roll(moved, (t - v) * span % LANES, 1)
                value = jnp.where(owner == t, moved, value)
            field[v, g * local : (g + 1) * local, :] = value[:local]
        row = jnp.broadcast_to(blocks[0][local : local + 1], (TILE, LANES))
        for v in range(reach):
            w = jnp.sum(jnp.where(lane == sub * reach + v, row, 0.0), axis=1, keepdims=True)
            w = jnp.broadcast_to(w, (TILE, LANES))
            weight[v, g * local : (g + 1) * local, :] = w[:local]

    total = groups * local
    spot = lax.broadcasted_iota(jnp.int32, (total, LANES), 1) % half
    across = spot % grid_cols
    down = spot // grid_cols
    one = lambda mask: mask.astype(jnp.float32)
    left, right = one(across > 0), one(across < grid_cols - 1)
    up, below = one(down > 0), one(down < grid_rows - 1)

    def sweep(_, u):
        plane = (
            up * (pltpu.roll(u, grid_cols, 1) - u)
            + below * (pltpu.roll(u, LANES - grid_cols, 1) - u)
            + left * (pltpu.roll(u, 1, 1) - u)
            + right * (pltpu.roll(u, LANES - 1, 1) - u)
        )
        spring = jnp.zeros_like(u)
        for v in range(reach):
            o = v + 1
            r = weight[v] * (pltpu.roll(u, total - o, 0) - u - field[v])
            spring = spring + r - pltpu.roll(r, o, 0)
        return u + STEP_SIZE * (plane + spring)

    state = lax.fori_loop(0, SWEEPS, sweep, field[reach])
    field[reach] = state
    mine = field[reach, pl.ds(sec * local, local), :]
    mine = jnp.concatenate([mine, jnp.zeros((TILE - local, LANES), jnp.float32)], axis=0)
    out[...] = pltpu.roll(mine, (LANES - tile * span) % LANES, 1)


def shards(patches, pair_flags, nodes):
    local, rows, cols, n = patches.shape[:4]
    reach = pair_flags.shape[1]
    groups, tiles = lax.axis_size("sec"), lax.axis_size("tile")
    part = n // 2 + TILE
    tab = jnp.asarray(tables(n))
    back_by_one = [(i, i - 1) for i in range(1, groups)]
    head = patches[: reach - 1]
    early = lax.ppermute(head, "sec", back_by_one)
    _, rest = lax.optimization_barrier((head, patches))
    late = lax.ppermute(rest[reach - 1 : reach], "sec", back_by_one)

    patch_block = (1, 1, cols, n, n)
    red, tail, edge = pl.pallas_call(
        functools.partial(own_kernel, reach),
        grid=(local,),
        in_specs=[pl.BlockSpec((1, rows, cols, n, n), lambda s: (s, 0, 0, 0, 0))] + [fixed(tab)],
        out_specs=[
            pl.BlockSpec((local, reach, rows, TILE, 2 * cols), lambda s: (0, 0, 0, 0, 0)),
            pl.BlockSpec((reach, rows, cols, 2 * part, n), lambda s: (0, 0, 0, 0, 0)),
            pl.BlockSpec((1, rows, cols, 2 * part, n), lambda s: (0, 0, 0, 0, 0)),
        ],
        out_shape=[
            jax.ShapeDtypeStruct((local, reach, rows, TILE, 2 * cols), jnp.float32),
            jax.ShapeDtypeStruct((reach, rows, cols, 2 * part, n), jnp.bfloat16),
            jax.ShapeDtypeStruct((1, rows, cols, 2 * part, n), jnp.bfloat16),
        ],
        scratch_shapes=[
            pltpu.VMEM((local, rows, cols, 2 * part, n), jnp.float32),
            pltpu.VMEM((rows, 2 * cols, n), jnp.float32),
        ],
        compiler_params=pltpu.CompilerParams(
            dimension_semantics=("arbitrary",), vmem_limit_bytes=40 << 20
        ),
        cost_estimate=cost(local * rows * cols, (reach * local - reach * (reach + 1) // 2) * rows * cols, n),
        name="own_pairs",
    )(patches, tab)

    grid = {}
    for r in range(reach - 1):
        count = reach - r
        own_specs = [
            pl.BlockSpec((1, 1, cols, 2 * part, n), functools.partial(lambda k, i: (k, i, 0, 0, 0), k))
            for k in range(r, reach)
        ]
        far_call = pl.pallas_call(
            functools.partial(far_kernel, count),
            grid=(rows,),
            in_specs=[pl.BlockSpec(patch_block, functools.partial(lambda k, i: (k, i, 0, 0, 0), r))] + [fixed(tab)] + own_specs,
            out_specs=pl.BlockSpec((count, 1, TILE, 2 * cols), lambda i: (0, i, 0, 0)),
            out_shape=jax.ShapeDtypeStruct((count, rows, TILE, 2 * cols), jnp.float32),
            scratch_shapes=[
                pltpu.VMEM((cols, 2 * part, n), jnp.float32),
                pltpu.VMEM((2 * cols, n), jnp.float32),
            ],
            compiler_params=pltpu.CompilerParams(
                dimension_semantics=("arbitrary",), vmem_limit_bytes=24 << 20
            ),
            cost_estimate=cost(rows * cols, count * rows * cols, n),
        )
        far = far_call(early, tab, *([tail] * count))
        for item in range(count):
            section = local - reach + r + item
            grid[section, local + r - section] = far[item]
    stats = jnp.stack(
        [
            jnp.stack([grid.get((s, o), red[s, o - 1]) for o in range(1, reach + 1)], 0)
            for s in range(local)
        ],
        0,
    )

    placed = lax.axis_index("sec") * local + jnp.arange(local, dtype=jnp.int32)
    offsets = jnp.arange(1, reach + 1, dtype=jnp.int32)
    weights = pair_flags.astype(jnp.float32) * (
        placed[:, None] + offsets[None, :] < groups * local
    ).astype(jnp.float32)
    area = float(n * n)
    total = stats[..., 0, cols:] / area + EPSILON
    ratio = jnp.stack([stats[..., 0, :cols], stats[..., 1, cols:]], 0) / area / total
    measured = ratio * weights[None, :, :, None, None]

    span = rows * cols
    lanes = jnp.concatenate(
        [
            jnp.transpose(measured, (1, 0, 2, 3, 4)).reshape(local, 2, reach * span),
            jnp.transpose(nodes, (1, 0, 2, 3)).reshape(local, 2, span),
        ],
        axis=2,
    )
    lanes = jnp.pad(lanes, ((0, 0), (0, 0), (0, LANES // 2 - (reach + 1) * span)))
    flat = jnp.pad(weights.reshape(1, local * reach), ((0, 0), (0, LANES - local * reach)))
    base = jnp.concatenate([lanes.reshape(local, LANES), flat], axis=0)
    base = jnp.pad(base, ((0, TILE - local - 1), (0, 0)))

    sizes = (groups, tiles, local, reach, span, tiles * rows, cols)
    vmem = pl.BlockSpec(memory_space=pltpu.VMEM)
    moved, payload = pl.pallas_call(
        functools.partial(relax_kernel, sizes),
        in_specs=[vmem] * 4,
        out_specs=[vmem, vmem],
        out_shape=[jax.ShapeDtypeStruct((TILE, LANES), jnp.float32)] * 2,
        scratch_shapes=[
            pltpu.VMEM((groups * tiles, TILE, LANES), jnp.float32),
            pltpu.VMEM((reach + 1, groups * local, LANES), jnp.float32),
            pltpu.VMEM((reach, groups * local, LANES), jnp.float32),
            pltpu.VMEM((rows, cols, 2 * part, n), jnp.float32),
            pltpu.VMEM((rows, 2 * cols, n), jnp.float32),
            pltpu.SemaphoreType.DMA((groups * tiles,)),
            pltpu.SemaphoreType.DMA((groups * tiles,)),
        ],
        compiler_params=pltpu.CompilerParams(
            collective_id=0, has_side_effects=True, vmem_limit_bytes=24 << 20
        ),
        name="relax",
    )(base, late, tab, edge)
    measured = payload[:local].reshape(local, 2, LANES // 2)[:, :, : reach * span]
    measured = jnp.transpose(measured.reshape(local, 2, reach, rows, cols), (1, 0, 2, 3, 4))
    positions = moved[:local].reshape(local, 2, LANES // 2)[:, :, :span]
    positions = jnp.transpose(positions.reshape(local, 2, rows, cols), (1, 0, 2, 3))
    return (positions, measured)


def solution(mesh):
    placed = (P("sec", "tile", None, None, None), P("sec", None), P(None, "sec", "tile", None))
    return jax.shard_map(
        shards,
        mesh=mesh,
        in_specs=placed,
        out_specs=(P(None, "sec", "tile", None), P(None, "sec", None, "tile", None)),
        check_vma=False,
    )
```

```python
import functools
import math

import jax
import jax.numpy as jnp
import numpy as np
from jax import lax
from jax.experimental import pallas as pl
from jax.experimental.pallas import tpu as pltpu
from jax.sharding import PartitionSpec as P


SWEEPS = 8
STEP_SIZE = 0.08
EPSILON = 1e-06
LANES = 128
TILE = 8
MESH = pl.DeviceIdType.MESH


def tables(n):
    h = n // 2
    k = np.arange(n)
    phase = (k[:, None] * k[None, :] % n) * (2.0 * math.pi / n)
    c = np.asarray(np.cos(phase), np.float32).astype(jnp.bfloat16).astype(np.float32)
    s = np.asarray(np.sin(phase), np.float32).astype(jnp.bfloat16).astype(np.float32)
    part = h + TILE
    first = np.zeros((2 * part, 2 * n), np.float32)
    first[: h + 1, :n] = c[: h + 1]
    first[part : part + h, :n] = s[:h]
    second = np.concatenate([np.concatenate([c, -s], 1), np.concatenate([-s, -c], 1)], 0)
    inverse = np.concatenate([np.concatenate([c, s], 1), np.concatenate([-s, c], 1)], 0)
    order = (np.arange(n) - h) % n
    last = np.zeros((n, 2 * n), np.float32)
    last[:, 0] = c[order, 0]
    last[:, 1:h] = 2.0 * c[order, 1:h]
    last[:, h] = c[order, h]
    last[:, h + 1 : n] = -2.0 * s[order, 1:h]
    last *= 1.0 / float(n) ** 3
    return np.concatenate([first, second, inverse, last], 0).astype(jnp.bfloat16)


def open_tables(tab, n):
    part = n // 2 + TILE
    first = tab[: 2 * part, :n]
    second = tab[2 * part : 2 * part + 2 * n]
    inverse = tab[2 * part + 2 * n : 2 * part + 4 * n]
    last = tab[2 * part + 4 * n :, :n]
    sub = lax.broadcasted_iota(jnp.int32, (TILE, n), 0)
    lane = lax.broadcasted_iota(jnp.int32, (TILE, n), 1)
    shift = jnp.where(lane < n // 2, lane, lane - n).astype(jnp.float32)
    weigh = jnp.where(sub == 0, 1.0, jnp.where(sub == 1, shift, 0.0))
    return (first, second), (inverse, last, weigh)


def spectra(x, first, second, put):
    cols, n = x.shape[0], x.shape[-1]
    part = n // 2 + TILE
    lines = []
    for c in range(0, cols, 2):
        y = jnp.dot(
            first, jnp.concatenate([x[c], x[c + 1]], axis=1), preferred_element_type=jnp.float32
        )
        for d in (0, 1):
            mine = y[:, d * n : (d + 1) * n]
            lines.append(jnp.concatenate([mine[:part], mine[part:]], axis=1))
    lines = jnp.concatenate(lines, axis=0).astype(jnp.bfloat16)
    spec = jnp.dot(lines, second, preferred_element_type=jnp.float32)
    for c in range(cols):
        mine = spec[c * part : (c + 1) * part]
        put(c, mine[:, :n], mine[:, n:])


def pairs(get_a, get_b, cols, n, inverse, last, weigh, sums):
    h = n // 2
    part = h + TILE
    crosses = []
    for c in range(cols):
        a, b = get_a(c), get_b(c)
        ar, ai, br, bi = a[:part], a[part:], b[:part], b[part:]
        real = ar * br + ai * bi
        imag = ar * bi - ai * br
        real_top = real[:TILE] - imag[h:]
        imag_top = imag[:TILE] + real[h:]
        real = jnp.concatenate([real_top, real[TILE:h]], axis=0).astype(jnp.bfloat16)
        imag = jnp.concatenate([imag_top, imag[TILE:h]], axis=0).astype(jnp.bfloat16)
        crosses.append(jnp.concatenate([real, imag], axis=1))
    back = jnp.dot(
        jnp.concatenate(crosses, axis=0), inverse, preferred_element_type=jnp.float32
    ).astype(jnp.bfloat16)
    place = lax.broadcasted_iota(jnp.int32, (TILE, 1), 0).astype(jnp.float32) + float(h)
    for c in range(0, cols, 2):
        sides = []
        for d in (c, c + 1):
            mine = back[d * h : (d + 1) * h]
            sides.append(jnp.concatenate([mine[:, :n], mine[:, n:]], axis=0))
        corr = jnp.dot(last, jnp.concatenate(sides, axis=1), preferred_element_type=jnp.float32)
        power = corr * corr
        total = power[:TILE]
        ramp = total
        for t in range(1, n // TILE):
            total = total + power[t * TILE : (t + 1) * TILE]
            ramp = ramp + total
        shifted = place * total - float(TILE) * ramp
        total = jnp.sum(total, axis=0, keepdims=True)
        shifted = jnp.sum(shifted, axis=0, keepdims=True)
        for d in (0, 1):
            sums[c + d : c + d + 1, :] = shifted[:, d * n : (d + 1) * n]
            sums[cols + c + d : cols + c + d + 1, :] = total[:, d * n : (d + 1) * n]
    return lax.dot_general(
        weigh,
        sums[...],
        (((1,), (1,)), ((), ())),
        precision=lax.Precision.HIGHEST,
        preferred_element_type=jnp.float32,
    )


def own_kernel(reach, x, tab, red, tail, edge, spec, sums):
    step = pl.program_id(0)
    local = pl.num_programs(0)
    rows, cols, n = x.shape[1], x.shape[2], x.shape[-1]

    part = n // 2 + TILE
    forward, inverse = open_tables(tab, n)

    for row in range(rows):

        def put(c, real, imag):
            spec[step, row, c, :part] = real
            spec[step, row, c, part:] = imag

        spectra(x.at[0, row], *forward, put)

    @pl.when(step >= local - reach)
    def _():
        tail[jnp.maximum(step - (local - reach), 0)] = spec[step].astype(tail.dtype)

    @pl.when(step == local - 1)
    def _():
        edge[0] = spec[step].astype(edge.dtype)

    def body(offset, carry):
        for row in range(rows):
            red[step - offset, offset - 1, row] = pairs(
                lambda c: spec[step - offset, row, c],
                lambda c: spec[step, row, c],
                cols, n, *inverse, sums.at[row],
            )
        return carry

    lax.fori_loop(1, jnp.minimum(step, reach) + 1, body, 0)


def far_kernel(count, x, tab, *rest):
    own, red, spec, sums = rest[:count], rest[count], rest[count + 1], rest[count + 2]
    cols, n = x.shape[2], x.shape[-1]

    part = n // 2 + TILE
    forward, inverse = open_tables(tab, n)

    def put(c, real, imag):
        spec[c, :part] = real
        spec[c, part:] = imag

    spectra(x.at[0, 0], *forward, put)
    for item in range(count):
        red[item, 0] = pairs(
            lambda c: own[item][0, 0, c].astype(jnp.float32),
            lambda c: spec[c],
            cols, n, *inverse, sums,
        )


def fixed(array):
    zeros = (0,) * array.ndim
    return pl.BlockSpec(array.shape, lambda *_: zeros)


def cost(patches, pair_count, n):
    return pl.CostEstimate(
        flops=(patches + pair_count) * 24 * n**3,
        bytes_accessed=patches * n * n * 16,
        transcendentals=0,
    )


def relax_kernel(
    sizes, base, late, tab, edge, out, payload, slots, field, weight, spec, tail, sums, local_sem, send, recv
):
    groups, tiles, local, reach, span, grid_rows, grid_cols = sizes
    half = LANES // 2
    sec = lax.axis_index("sec")
    tile = lax.axis_index("tile")
    me = sec * tiles + tile
    count = groups * tiles
    unroll = count <= 64

    def place(index):
        return (index // tiles, index % tiles)

    fetch = pltpu.make_async_copy(edge, tail, local_sem)
    fetch.start()
    barrier = pltpu.get_barrier_semaphore()

    def greet(d, carry):
        pl.semaphore_signal(
            barrier, inc=1, device_id=place((me + d) % count), device_id_type=MESH
        )
        return carry

    lax.fori_loop(1, count, greet, 0, unroll=unroll)

    rows, cols, n = late.shape[1], late.shape[2], late.shape[-1]
    part = n // 2 + TILE
    forward, inverse = open_tables(tab, n)
    for row in range(rows):

        def put(c, real, imag):
            spec[row, c, :part] = real
            spec[row, c, part:] = imag

        spectra(late.at[0, row], *forward, put)
    fetch.wait()
    payload[...] = base[...]
    key = (local - 1) * reach + reach - 1
    flag = base[local : local + 1, key : key + 1]
    for row in range(rows):
        red = pairs(
            lambda c: tail[0, row, c].astype(jnp.float32),
            lambda c: spec[row, c],
            cols, n, *inverse, sums.at[row],
        )
        area = float(n * n)
        scale = flag / (red[:1, cols:] / area + EPSILON)
        at = (reach - 1) * span + row * cols
        payload[local - 1 : local, at : at + cols] = red[:1, :cols] / area * scale
        payload[local - 1 : local, half + at : half + at + cols] = red[1:2, cols:] / area * scale
    pl.semaphore_wait(barrier, count - 1)

    def copy(slot, peer):
        return pltpu.make_async_remote_copy(
            src_ref=payload,
            dst_ref=slots.at[slot],
            send_sem=send.at[peer],
            recv_sem=recv.at[slot],
            device_id=place(peer),
            device_id_type=MESH,
        )

    def start(d, carry):
        copy(me, (me + d) % count).start()
        return carry

    lax.fori_loop(1, count, start, 0, unroll=unroll)
    slots[me] = payload[...]

    def finish(d, carry):
        peer = (me + d) % count
        copy(peer, peer).wait_recv()
        copy(me, peer).wait_send()
        return carry

    lax.fori_loop(1, count, finish, 0, unroll=unroll)

    lane = lax.broadcasted_iota(jnp.int32, (TILE, LANES), 1)
    sub = lax.broadcasted_iota(jnp.int32, (TILE, LANES), 0)
    owner = lane % half // span
    for g in range(groups):
        blocks = [slots[g * tiles + t] for t in range(tiles)]
        for v in range(reach + 1):
            value = jnp.zeros((TILE, LANES), jnp.float32)
            for t in range(tiles):
                moved = blocks[t]
                if t != v:
                    moved = pltpu.roll(moved, (t - v) * span % LANES, 1)
                value = jnp.where(owner == t, moved, value)
            field[v, g * local : (g + 1) * local, :] = value[:local]
        row = jnp.broadcast_to(blocks[0][local : local + 1], (TILE, LANES))
        for v in range(reach):
            w = jnp.sum(jnp.where(lane == sub * reach + v, row, 0.0), axis=1, keepdims=True)
            w = jnp.broadcast_to(w, (TILE, LANES))
            weight[v, g * local : (g + 1) * local, :] = w[:local]

    total = groups * local
    spot = lax.broadcasted_iota(jnp.int32, (total, LANES), 1) % half
    across = spot % grid_cols
    down = spot // grid_cols
    one = lambda mask: mask.astype(jnp.float32)
    left, right = one(across > 0), one(across < grid_cols - 1)
    up, below = one(down > 0), one(down < grid_rows - 1)

    def sweep(_, u):
        plane = (
            up * (pltpu.roll(u, grid_cols, 1) - u)
            + below * (pltpu.roll(u, LANES - grid_cols, 1) - u)
            + left * (pltpu.roll(u, 1, 1) - u)
            + right * (pltpu.roll(u, LANES - 1, 1) - u)
        )
        spring = jnp.zeros_like(u)
        for v in range(reach):
            o = v + 1
            r = weight[v] * (pltpu.roll(u, total - o, 0) - u - field[v])
            spring = spring + r - pltpu.roll(r, o, 0)
        return u + STEP_SIZE * (plane + spring)

    state = lax.fori_loop(0, SWEEPS, sweep, field[reach])
    field[reach] = state
    mine = field[reach, pl.ds(sec * local, local), :]
    mine = jnp.concatenate([mine, jnp.zeros((TILE - local, LANES), jnp.float32)], axis=0)
    out[...] = pltpu.roll(mine, (LANES - tile * span) % LANES, 1)


def shards(patches, pair_flags, nodes):
    local, rows, cols, n = patches.shape[:4]
    reach = pair_flags.shape[1]
    groups, tiles = lax.axis_size("sec"), lax.axis_size("tile")
    part = n // 2 + TILE
    tab = jnp.asarray(tables(n))
    back_by_one = [(i, i - 1) for i in range(1, groups)]
    ahead = []
    source = patches
    for r in range(reach):
        piece = source[r : r + 1]
        ahead.append(lax.ppermute(piece, "sec", back_by_one))
        _, source = lax.optimization_barrier((piece, source))

    patch_block = (1, 1, cols, n, n)
    own_call = pl.pallas_call(
        functools.partial(own_kernel, reach),
        grid=(local,),
        in_specs=[pl.BlockSpec((1, rows, cols, n, n), lambda s: (s, 0, 0, 0, 0))] + [fixed(tab)],
        out_specs=[
            pl.BlockSpec((local, reach, rows, TILE, 2 * cols), lambda s: (0, 0, 0, 0, 0)),
            pl.BlockSpec((reach, rows, cols, 2 * part, n), lambda s: (0, 0, 0, 0, 0)),
            pl.BlockSpec((1, rows, cols, 2 * part, n), lambda s: (0, 0, 0, 0, 0)),
        ],
        out_shape=[
            jax.ShapeDtypeStruct((local, reach, rows, TILE, 2 * cols), jnp.float32),
            jax.ShapeDtypeStruct((reach, rows, cols, 2 * part, n), jnp.bfloat16),
            jax.ShapeDtypeStruct((1, rows, cols, 2 * part, n), jnp.bfloat16),
        ],
        scratch_shapes=[
            pltpu.VMEM((local, rows, cols, 2 * part, n), jnp.float32),
            pltpu.VMEM((rows, 2 * cols, n), jnp.float32),
        ],
        compiler_params=pltpu.CompilerParams(
            dimension_semantics=("arbitrary",), vmem_limit_bytes=40 << 20
        ),
        cost_estimate=cost(local * rows * cols, (reach * local - reach * (reach + 1) // 2) * rows * cols, n),
        name="own_pairs",
    )
    red, tail, edge = own_call(patches, tab)

    grid = {}
    for r in range(reach - 1):
        count = reach - r
        own_specs = [
            pl.BlockSpec((1, 1, cols, 2 * part, n), functools.partial(lambda k, i: (k, i, 0, 0, 0), k))
            for k in range(r, reach)
        ]
        far_call = pl.pallas_call(
            functools.partial(far_kernel, count),
            grid=(rows,),
            in_specs=[pl.BlockSpec(patch_block, lambda i: (0, i, 0, 0, 0))] + [fixed(tab)] + own_specs,
            out_specs=pl.BlockSpec((count, 1, TILE, 2 * cols), lambda i: (0, i, 0, 0)),
            out_shape=jax.ShapeDtypeStruct((count, rows, TILE, 2 * cols), jnp.float32),
            scratch_shapes=[
                pltpu.VMEM((cols, 2 * part, n), jnp.float32),
                pltpu.VMEM((2 * cols, n), jnp.float32),
            ],
            compiler_params=pltpu.CompilerParams(
                dimension_semantics=("arbitrary",), vmem_limit_bytes=24 << 20
            ),
            cost_estimate=cost(rows * cols, count * rows * cols, n),
        )
        far = far_call(ahead[r], tab, *([tail] * count))
        for item in range(count):
            section = local - reach + r + item
            grid[section, local + r - section] = far[item]
    stats = jnp.stack(
        [
            jnp.stack([grid.get((s, o), red[s, o - 1]) for o in range(1, reach + 1)], 0)
            for s in range(local)
        ],
        0,
    )

    placed = lax.axis_index("sec") * local + jnp.arange(local, dtype=jnp.int32)
    offsets = jnp.arange(1, reach + 1, dtype=jnp.int32)
    weights = pair_flags.astype(jnp.float32) * (
        placed[:, None] + offsets[None, :] < groups * local
    ).astype(jnp.float32)
    area = float(n * n)
    total = stats[..., 0, cols:] / area + EPSILON
    ratio = jnp.stack([stats[..., 0, :cols], stats[..., 1, cols:]], 0) / area / total
    measured = ratio * weights[None, :, :, None, None]

    span = rows * cols
    lanes = jnp.concatenate(
        [
            jnp.transpose(measured, (1, 0, 2, 3, 4)).reshape(local, 2, reach * span),
            jnp.transpose(nodes, (1, 0, 2, 3)).reshape(local, 2, span),
        ],
        axis=2,
    )
    lanes = jnp.pad(lanes, ((0, 0), (0, 0), (0, LANES // 2 - (reach + 1) * span)))
    flat = jnp.pad(weights.reshape(1, local * reach), ((0, 0), (0, LANES - local * reach)))
    base = jnp.concatenate([lanes.reshape(local, LANES), flat], axis=0)
    base = jnp.pad(base, ((0, TILE - local - 1), (0, 0)))

    sizes = (groups, tiles, local, reach, span, tiles * rows, cols)
    vmem = pl.BlockSpec(memory_space=pltpu.VMEM)
    moved, payload = pl.pallas_call(
        functools.partial(relax_kernel, sizes),
        in_specs=[vmem] * 3 + [pl.BlockSpec(memory_space=pltpu.HBM)],
        out_specs=[vmem, vmem],
        out_shape=[jax.ShapeDtypeStruct((TILE, LANES), jnp.float32)] * 2,
        scratch_shapes=[
            pltpu.VMEM((groups * tiles, TILE, LANES), jnp.float32),
            pltpu.VMEM((reach + 1, groups * local, LANES), jnp.float32),
            pltpu.VMEM((reach, groups * local, LANES), jnp.float32),
            pltpu.VMEM((rows, cols, 2 * part, n), jnp.float32),
            pltpu.VMEM((1, rows, cols, 2 * part, n), jnp.bfloat16),
            pltpu.VMEM((rows, 2 * cols, n), jnp.float32),
            pltpu.SemaphoreType.DMA,
            pltpu.SemaphoreType.DMA((groups * tiles,)),
            pltpu.SemaphoreType.DMA((groups * tiles,)),
        ],
        compiler_params=pltpu.CompilerParams(
            collective_id=0, has_side_effects=True, vmem_limit_bytes=24 << 20
        ),
        name="relax",
    )(base, ahead[-1], tab, edge)
    measured = payload[:local].reshape(local, 2, LANES // 2)[:, :, : reach * span]
    measured = jnp.transpose(measured.reshape(local, 2, reach, rows, cols), (1, 0, 2, 3, 4))
    positions = moved[:local].reshape(local, 2, LANES // 2)[:, :, :span]
    positions = jnp.transpose(positions.reshape(local, 2, rows, cols), (1, 0, 2, 3))
    return (positions, measured)


def solution(mesh):
    placed = (P("sec", "tile", None, None, None), P("sec", None), P(None, "sec", "tile", None))
    return jax.shard_map(
        shards,
        mesh=mesh,
        in_specs=placed,
        out_specs=(P(None, "sec", "tile", None), P(None, "sec", None, "tile", None)),
        check_vma=False,
    )
```
